256 devices in a mesh: node: 16 (over z, core), trow: 4 (over x), tcol: 4 (over y).
Axes of the slice: x: 4, y: 4, z: 8, core: 2. Of those that a mesh axis runs over, the one named last changes fastest.
Arguments:
- near_blocks: bfloat16 [1024, 8, 256, 256], P(('node', 'trow'), 'tcol'), may hold values from -27 to 75, as said below
- leaf_bases: bfloat16 [1024, 256, 256], P(('node', 'trow')), may hold values from -1 to 1, as said below
- upper_bases: bfloat16 [512, 256, 256], P(('node', 'trow', 'tcol')), may hold values from -1 to 1, as said below
- neighbours: int32 [1024, 8], P(('node', 'trow'), 'tcol'), may hold values from 0 to 1023, as said below
Outputs:
- skeleton: float32 [1024, 8, 128, 128], P(('node', 'trow'), 'tcol')
- upper_skeleton: float32 [512, 5, 128, 128], P(('node', 'trow', 'tcol'))
The draws below stay inside these ranges and needn't reach their ends.
Inputs may be any that keep to these rules, and one draw needn't show every extreme that they name: `neighbours`: slot 0 of row i is i, slot 1 is its sibling i XOR 1, and slots 2 to 7 are six distinct leaves among 2 (i // 2) - 4, -3, -2, -1, +2, +3, +4, +5, taken modulo 1024. near_blocks[i, 0] is symmetric and positive definite. `leaf_bases`: each leaf basis is an orthogonal matrix rounded to bfloat16. `upper_bases`: each node basis is an orthogonal matrix rounded to bfloat16.
All inputs are finite; a program needn't handle non-finite values.
Results may differ from the reference program's by a relative error of at most 0.0038.
Values may be sent and summed in bfloat16 or wider, within the bound.
A program may use at most 64 MiB of HBM per device.

```python
import math
import jax
import jax.numpy as jnp
from jax import lax

BLK = 256
RANK = 128
LEAVES = 1024
PARENTS = 512


def draw_near_blocks(key, part):
    first_key = jax.random.fold_in(jax.random.fold_in(key, 11), 0)
    frame_key = jax.random.fold_in(key, 31)
    level_key = jax.random.fold_in(key, 37)
    shape = (LEAVES, 8, BLK, BLK)
    root = math.sqrt(BLK)
    noise = 0.5 * jnp.clip(jax.random.normal(first_key, shape, jnp.float32), -4.0, 4.0)
    levels = root * jax.random.uniform(level_key, (LEAVES, BLK), jnp.float32, 1.5, 4.5)
    frame_draw = jax.random.normal(frame_key, (LEAVES, BLK, BLK), jnp.float32)
    frame, upper = jnp.linalg.qr(frame_draw)
    graded = jnp.einsum('lab,lb,lcb->lac', frame, levels, frame, precision=lax.Precision.HIGHEST)
    graded = 0.5 * (graded + jnp.swapaxes(graded, 1, 2))
    diagonal = 0.5 * (noise[:, 0] + jnp.swapaxes(noise[:, 0], 1, 2)) + graded
    return noise.at[:, 0].set(diagonal).astype(jnp.bfloat16)


def orthogonal(key, count, order):
    normal_draw = jax.random.normal(key, (count, order, order), jnp.float32)
    basis, upper = jnp.linalg.qr(normal_draw)
    return basis.astype(jnp.bfloat16)


def draw_leaf_bases(key, part):
    return orthogonal(jax.random.fold_in(key, 17), LEAVES, BLK)


def draw_upper_bases(key, part):
    return orthogonal(jax.random.fold_in(key, 23), PARENTS, 2 * RANK)


def draw_neighbours(key, part):
    leaf_ids = jnp.arange(LEAVES, dtype=jnp.int32)
    base_key = jax.random.fold_in(key, 29)
    row_keys = jax.vmap(lambda leaf: jax.random.fold_in(base_key, leaf))(leaf_ids)
    orders = jax.vmap(lambda row_key: jax.random.permutation(row_key, 8))(row_keys)
    offsets = jnp.array([-4, -3, -2, -1, 2, 3, 4, 5], jnp.int32)
    starts = leaf_ids // 2 * 2
    picks = (starts[:, None] + offsets[orders[:, :6]]) % LEAVES
    return jnp.concatenate([leaf_ids[:, None], (leaf_ids ^ 1)[:, None], picks], axis=1).astype(jnp.int32)


def setup_inputs(seed: int = 0) -> dict:
    streams_of = jax.random.split(jax.random.key(seed), 5)
    near_blocks = draw_near_blocks(jax.random.fold_in(streams_of[4], 71), 0)
    leaf_bases = draw_leaf_bases(jax.random.fold_in(streams_of[4], 71), 0)
    upper_bases = draw_upper_bases(jax.random.fold_in(streams_of[4], 71), 0)
    neighbours = draw_neighbours(jax.random.fold_in(streams_of[4], 71), 0)
    return dict(near_blocks=near_blocks, leaf_bases=leaf_bases, upper_bases=upper_bases, neighbours=neighbours)


def eliminate(rotated, spare_size):
    corner = rotated[..., :spare_size, :spare_size]
    factor = jnp.linalg.cholesky(0.5 * (corner + jnp.swapaxes(corner, -1, -2)))
    coupled = lax.linalg.triangular_solve(factor, rotated[..., :spare_size, spare_size:], left_side=True, lower=True)
    return (factor, coupled)

def reduce_one(rotated, factor, coupled, spare_size):
    widened = jnp.broadcast_to(factor, (rotated.shape[0],) + factor.shape)
    solved = lax.linalg.triangular_solve(widened, rotated[:, :spare_size, spare_size:], left_side=True, lower=True)
    return rotated[:, spare_size:, spare_size:] - jnp.einsum('xr,kxs->krs', coupled, solved, precision=lax.Precision.HIGHEST)

def reference(near_blocks, leaf_bases, upper_bases, neighbours):
    spare_size = BLK - RANK

    def leaf_row(item):
        blocks_row, basis_row, leaf_list = item
        partner = leaf_bases[leaf_list].astype(jnp.float32)
        turned = jnp.einsum('kab,kbc->kac', blocks_row.astype(jnp.float32), partner, precision=lax.Precision.HIGHEST).astype(jnp.bfloat16)
        turned = lax.optimization_barrier(turned)
        rotated = jnp.einsum('ba,kbc->kac', basis_row.astype(jnp.float32), turned.astype(jnp.float32), precision=lax.Precision.HIGHEST)
        factor, coupled = eliminate(rotated[0], spare_size)
        return reduce_one(rotated, factor, coupled, spare_size)
    skeleton = lax.map(leaf_row, (near_blocks, leaf_bases, neighbours))
    packed = skeleton.astype(jnp.bfloat16)
    leaf_ids = jnp.arange(LEAVES, dtype=jnp.int32)
    target = 2 * ((neighbours // 2 - leaf_ids[:, None] // 2 + 2) % PARENTS) + neighbours % 2
    labels = jnp.arange(10, dtype=jnp.int32)
    parent_ids = jnp.arange(PARENTS, dtype=jnp.int32)

    def parent_row(item):
        parent, pair_blocks, pair_target, basis_row = item
        selector = (pair_target[:, :, None] == labels).astype(jnp.float32)
        blocks = jnp.einsum('akc,akxy->acxy', selector, pair_blocks.astype(jnp.float32), precision=lax.Precision.HIGHEST)
        merged = blocks.reshape(2, 5, 2, RANK, RANK).transpose(1, 0, 3, 2, 4).reshape(5, 2 * RANK, 2 * RANK).astype(jnp.bfloat16)
        merged = lax.optimization_barrier(merged)
        offsets = (parent + jnp.arange(5, dtype=jnp.int32) - 2) % PARENTS
        partners = upper_bases[offsets.astype(jnp.int32)].astype(jnp.float32)
        upper_mixed = jnp.einsum('dab,dbc->dac', merged.astype(jnp.float32), partners, precision=lax.Precision.HIGHEST).astype(jnp.bfloat16)
        upper_mixed = lax.optimization_barrier(upper_mixed)
        lifted = jnp.einsum('ba,dbc->dac', basis_row.astype(jnp.float32), upper_mixed.astype(jnp.float32), precision=lax.Precision.HIGHEST)
        factor, coupled = eliminate(lifted[2], RANK)
        return reduce_one(lifted, factor, coupled, RANK)
    upper_skeleton = lax.map(parent_row, (parent_ids, packed.reshape(PARENTS, 2, 8, RANK, RANK), target.reshape(PARENTS, 2, 8), upper_bases))
    return (skeleton, upper_skeleton)
```

```python
import functools

import jax
import jax.numpy as jnp
from jax import lax
from jax.experimental import pallas as pl
from jax.experimental.pallas import tpu as pltpu
from jax.sharding import PartitionSpec as P

BLK = 256
RANK = 128
PANEL = 16
BF = jnp.bfloat16
F32 = jnp.float32


def mm(a, b):
    return lax.dot_general(a, b, (((1,), (0,)), ((), ())), preferred_element_type=F32)


def mm_t(a, b):
    return lax.dot_general(a, b, (((0,), (0,)), ((), ())), preferred_element_type=F32)


def split3(x):
    high = x.astype(BF)
    rest = x - high.astype(F32)
    mid = rest.astype(BF)
    low = (rest - mid.astype(F32)).astype(BF)
    return high, mid, low


def mm_exact(a, b):
    ah, am, al = split3(a)
    bh, bm, bl = split3(b)
    left = jnp.concatenate([ah, ah, am, ah, am, al], axis=1)
    right = jnp.concatenate([bh, bm, bh, bl, bm, bh], axis=0)
    return mm(left, right)


def mm_exact_t(a, b):
    ah, am, al = split3(a)
    bh, bm, bl = split3(b)
    left = jnp.concatenate([ah, ah, am, ah, am, al], axis=0)
    right = jnp.concatenate([bh, bm, bh, bl, bm, bh], axis=0)
    return mm_t(left, right)


def sweep_panel(panel, start):
    lane = lax.broadcasted_iota(jnp.int32, panel.shape, 2)
    sub = lax.broadcasted_iota(jnp.int32, panel.shape, 1)
    for step in range(PANEL):
        here = lane == start + step
        column = jnp.broadcast_to(panel[:, :, start + step : start + step + 1], panel.shape)
        pivot = column[:, step : step + 1]
        row = jnp.where(here[:, :1], 1.0, panel[:, step : step + 1]) / pivot
        rest = jnp.where(here, 0.0, panel) - column * row
        panel = jnp.where(sub == step, row, rest)
    return panel


def sweep(matrix_ref, count, group):
    order = matrix_ref.shape[-1]
    lane = lax.broadcasted_iota(jnp.int32, (order, order), 1)
    lane_panel = lax.broadcasted_iota(jnp.int32, (PANEL, order), 1)
    for start in range(0, order, PANEL):
        for first in range(0, count, group):
            rows = matrix_ref[first : first + group, start : start + PANEL, :]
            swept = sweep_panel(rows, start)
            inside = (lane >= start) & (lane < start + PANEL)
            inside_panel = (lane_panel >= start) & (lane_panel < start + PANEL)
            for leaf in range(group):
                signed = jnp.where(inside_panel, -swept[leaf], swept[leaf])
                update = mm_exact_t(rows[leaf], signed)
                matrix_ref[first + leaf] = jnp.where(inside, 0.0, matrix_ref[first + leaf]) - update
                matrix_ref[first + leaf, start : start + PANEL, :] = signed


def leaf_gain_kernel(near_ref, base_ref, gain_ref, matrix_ref, right_ref):
    count = near_ref.shape[0]

    @pl.loop(0, count)
    def _(leaf):
        base = base_ref[leaf]
        turned = mm(near_ref[leaf], base).astype(BF)
        rotated = mm_t(base[:, :RANK], turned)
        corner = rotated[:, :RANK]
        matrix_ref[leaf] = 0.5 * (corner + corner.T)
        right_ref[leaf] = rotated[:, RANK:]

    sweep(matrix_ref, count, 8)

    @pl.loop(0, count)
    def _(leaf):
        gain_ref[leaf] = (-mm_exact(right_ref[leaf].T, matrix_ref[leaf])).astype(BF)


def rotate_kernel(place_ref, near_ref, base_ref, wide_ref, right_ref, low_ref):
    count = near_ref.shape[0]

    @pl.loop(0, count)
    def _(leaf):
        base = base_ref[leaf]
        turned = [
            mm(near_ref[leaf, slot], wide_ref[place_ref[leaf, slot]]).astype(BF)
            for slot in range(2)
        ]
        rotated = mm_t(base, jnp.concatenate(turned, axis=1))
        for slot in range(2):
            right_ref[leaf, slot] = rotated[:RANK, slot * RANK : (slot + 1) * RANK]
            low_ref[leaf, slot] = rotated[RANK:, slot * RANK : (slot + 1) * RANK]


def leaf_skeleton_kernel(right_ref, low_ref, gain_ref, skeleton_ref, packed_ref):
    count = right_ref.shape[0]

    @pl.loop(0, count)
    def _(leaf):
        gain = gain_ref[leaf]
        for slot in range(2):
            block = low_ref[leaf, slot] - mm(gain, right_ref[leaf, slot].astype(BF))
            skeleton_ref[leaf, slot] = block
            packed_ref[leaf, slot] = block.astype(BF)


def upper_kernel(target_ref, block_ref, base_ref, before_ref, after_ref, out_ref,
                 merged_ref, matrix_ref, right_ref, low_ref):
    parents = base_ref.shape[0]
    merged_ref[...] = jnp.zeros_like(merged_ref)
    for leaf in range(2 * parents):
        for slot in range(8):
            place = (leaf // 2) * 10 + target_ref[leaf, slot]
            rows = slice((leaf % 2) * RANK, (leaf % 2 + 1) * RANK)
            merged_ref[place, rows, :] = block_ref[leaf, slot]
    for p in range(parents):
        base = base_ref[p]
        for d in range(5):
            left = jnp.concatenate([merged_ref[p * 10 + 2 * d], merged_ref[p * 10 + 2 * d + 1]], axis=1)
            q = p + d - 2
            if d == 2:
                partner = base
            elif q < 0:
                partner = before_ref[q + parents]
            elif q >= parents:
                partner = after_ref[q - parents]
            else:
                partner = base_ref[q, :, RANK:]
            mixed = mm(left, partner).astype(BF)
            lifted = mm_t(base, mixed)
            if d == 2:
                corner = lifted[:RANK, :RANK]
                matrix_ref[p] = 0.5 * (corner + corner.T)
                lifted = lifted[:, RANK:]
            right_ref[p, d] = lifted[:RANK]
            low_ref[p, d] = lifted[RANK:]
    sweep(matrix_ref, parents, parents)
    for p in range(parents):
        gain = mm_exact(right_ref[p, 2].T, matrix_ref[p])
        for d in range(5):
            out_ref[p, d] = low_ref[p, d] + mm(gain.astype(BF), right_ref[p, d].astype(BF))


VM = pl.BlockSpec(memory_space=pltpu.VMEM)
SM = pl.BlockSpec(memory_space=pltpu.SMEM)
PARAMS = pltpu.CompilerParams(vmem_limit_bytes=48 * 1024 * 1024)


def shaped(shape, dtype):
    return jax.ShapeDtypeStruct(shape, dtype)


def leaf_gain(near, base):
    count = near.shape[0]
    return pl.pallas_call(
        leaf_gain_kernel,
        grid=(1,),
        in_specs=[pl.BlockSpec((count, None, BLK, BLK), lambda g: (0, 0, 0, 0)), VM],
        out_specs=VM,
        out_shape=shaped((count, RANK, RANK), BF),
        scratch_shapes=[pltpu.VMEM((count, RANK, RANK), F32)] * 2,
        compiler_params=PARAMS,
        name="leaf_gain",
    )(near, base)


def rotate(place, near, base, wide):
    count = near.shape[0]
    return pl.pallas_call(
        rotate_kernel,
        in_specs=[SM, VM, VM, VM],
        out_specs=[VM, VM],
        out_shape=[shaped((count, 2, RANK, RANK), F32)] * 2,
        compiler_params=PARAMS,
        name="rotate",
    )(place, near, base, wide)


def leaf_skeleton(right, low, gain):
    return pl.pallas_call(
        leaf_skeleton_kernel,
        in_specs=[VM] * 3,
        out_specs=[VM, VM],
        out_shape=[shaped(right.shape, F32), shaped(right.shape, BF)],
        compiler_params=PARAMS,
        name="leaf_skeleton",
    )(right, low, gain)


def upper(target, blocks, base, before, after):
    parents = base.shape[0]
    return pl.pallas_call(
        upper_kernel,
        in_specs=[SM] + [VM] * 4,
        out_specs=VM,
        out_shape=shaped((parents, 5, RANK, RANK), F32),
        scratch_shapes=[
            pltpu.VMEM((parents * 10, 2 * RANK, RANK), BF),
            pltpu.VMEM((parents, RANK, RANK), F32),
            pltpu.VMEM((parents, 5, RANK, RANK), F32),
            pltpu.VMEM((parents, 5, RANK, RANK), F32),
        ],
        compiler_params=PARAMS,
        name="upper",
    )(target, blocks, base, before, after)


def halo(last, initial, axis):
    count = lax.axis_size(axis)
    up = [(i, (i + 1) % count) for i in range(count)]
    down = [(j, i) for i, j in up]
    return lax.ppermute(last, axis, up), lax.ppermute(initial, axis, down)


def per_device(near_blocks, leaf_bases, upper_bases, neighbours):
    count = near_blocks.shape[0]
    total = count * lax.axis_size(("node", "trow"))
    first_leaf = lax.axis_index(("node", "trow")) * count
    skeleton_bases = leaf_bases[:, :, RANK:]
    before, after = halo(skeleton_bases[count - 4 :], skeleton_bases[:4], ("node", "trow"))
    upper_half = upper_bases[:, :, RANK:]
    upper_before, upper_after = halo(upper_half, upper_half, ("node", "trow", "tcol"))
    leaf_ids = first_leaf + jnp.arange(count, dtype=jnp.int32)
    target = 2 * ((neighbours // 2 - leaf_ids[:, None] // 2 + 2) % (total // 2)) + neighbours % 2
    arrived_target = lax.all_to_all(target, "tcol", split_axis=0, concat_axis=1, tiled=True)
    gain = leaf_gain(near_blocks, leaf_bases)
    sent = [lax.ppermute(gain, "tcol", [(0, j)]) for j in (1, 2, 3)]
    wide = jnp.concatenate([before, skeleton_bases, after], axis=0)
    place = (neighbours - first_leaf + total // 2) % total - total // 2 + 4
    right, low = rotate(place, near_blocks, leaf_bases, wide)
    mine = lax.axis_index("tcol")
    for j in (1, 2, 3):
        gain = jnp.where(mine == j, sent[j - 1], gain)
    skeleton, packed = leaf_skeleton(right, low, gain)
    arrived = lax.all_to_all(packed, "tcol", split_axis=0, concat_axis=1, tiled=True)
    upper_skeleton = upper(arrived_target, arrived, upper_bases, upper_before, upper_after)
    return (skeleton, upper_skeleton)


def solution(mesh):
    return jax.shard_map(
        per_device,
        mesh=mesh,
        in_specs=(
            P(("node", "trow"), "tcol", None, None),
            P(("node", "trow"), None, None),
            P(("node", "trow", "tcol"), None, None),
            P(("node", "trow"), "tcol"),
        ),
        out_specs=(
            P(("node", "trow"), "tcol", None, None),
            P(("node", "trow", "tcol"), None, None, None),
        ),
        check_vma=False,
    )
```

```python
import functools

import jax
import jax.numpy as jnp
from jax import lax
from jax.experimental import pallas as pl
from jax.experimental.pallas import tpu as pltpu
from jax.sharding import PartitionSpec as P

BLK = 256
RANK = 128
PANEL = 16
SHARE = 4
MESH = pl.DeviceIdType.MESH
BF = jnp.bfloat16
F32 = jnp.float32


def mm(a, b):
    return lax.dot_general(a, b, (((1,), (0,)), ((), ())), preferred_element_type=F32)


def mm_t(a, b):
    return lax.dot_general(a, b, (((0,), (0,)), ((), ())), preferred_element_type=F32)


def split3(x):
    high = x.astype(BF)
    rest = x - high.astype(F32)
    mid = rest.astype(BF)
    low = (rest - mid.astype(F32)).astype(BF)
    return high, mid, low


def mm_exact(a, b):
    ah, am, al = split3(a)
    bh, bm, bl = split3(b)
    left = jnp.concatenate([ah, ah, am, ah, am, al], axis=1)
    right = jnp.concatenate([bh, bm, bh, bl, bm, bh], axis=0)
    return mm(left, right)


def mm_exact_t(a, b):
    ah, am, al = split3(a)
    bh, bm, bl = split3(b)
    left = jnp.concatenate([ah, ah, am, ah, am, al], axis=0)
    right = jnp.concatenate([bh, bm, bh, bl, bm, bh], axis=0)
    return mm_t(left, right)


def sweep_panel(panel, start):
    lane = lax.broadcasted_iota(jnp.int32, panel.shape, 2)
    sub = lax.broadcasted_iota(jnp.int32, panel.shape, 1)
    for step in range(PANEL):
        here = lane == start + step
        column = jnp.broadcast_to(panel[:, :, start + step : start + step + 1], panel.shape)
        pivot = column[:, step : step + 1]
        row = jnp.where(here[:, :1], 1.0, panel[:, step : step + 1]) / pivot
        rest = jnp.where(here, 0.0, panel) - column * row
        panel = jnp.where(sub == step, row, rest)
    return panel


def sweep_panel_by_four(panel, start):
    parts = [panel[:, 8 * h : 8 * h + 8] for h in range(PANEL // 8)]
    shape = parts[0].shape
    lane = lax.broadcasted_iota(jnp.int32, (1,) + shape[1:], 2)
    sub = lax.broadcasted_iota(jnp.int32, (1,) + shape[1:], 1)

    def spread_row(x, row):
        return jnp.broadcast_to(x[:, row : row + 1], shape)

    for step in range(0, PANEL, 4):
        home, k = divmod(step, 8)
        s = start + step
        inside = (lane >= s) & (lane < s + 4)
        columns = [
            [jnp.broadcast_to(x[:, :, s + t : s + t + 1], shape) for x in parts] for t in range(4)
        ]
        e = {
            (i, j): spread_row(columns[j][home], k + i) for j in range(4) for i in range(j + 1)
        }
        r = [
            jnp.where(inside, jnp.where(lane == s + t, 1.0, 0.0), spread_row(parts[home], k + t))
            for t in range(4)
        ]
        first = 1.0 / (e[0, 0] * e[1, 1] - e[0, 1] * e[0, 1])

        def solve(p, q):
            return (e[1, 1] * p - e[0, 1] * q) * first, (e[0, 0] * q - e[0, 1] * p) * first

        u2, v2 = solve(e[0, 2], e[1, 2])
        u3, v3 = solve(e[0, 3], e[1, 3])
        s22 = e[2, 2] - (e[0, 2] * u2 + e[1, 2] * v2)
        s23 = e[2, 3] - (e[0, 2] * u3 + e[1, 2] * v3)
        s33 = e[3, 3] - (e[0, 3] * u3 + e[1, 3] * v3)
        second = 1.0 / (s22 * s33 - s23 * s23)
        t2 = r[2] - (u2 * r[0] + v2 * r[1])
        t3 = r[3] - (u3 * r[0] + v3 * r[1])
        n2 = (s33 * t2 - s23 * t3) * second
        n3 = (s22 * t3 - s23 * t2) * second
        m0, m1 = solve(r[0], r[1])
        n = [m0 - (u2 * n2 + u3 * n3), m1 - (v2 * n2 + v3 * n3), n2, n3]
        fresh = []
        for h, x in enumerate(parts):
            y = jnp.where(inside, 0.0, x) - (
                (columns[0][h] * n[0] + columns[1][h] * n[1])
                + (columns[2][h] * n[2] + columns[3][h] * n[3])
            )
            if h == home:
                for t in range(4):
                    y = jnp.where(sub == k + t, n[t], y)
            fresh.append(y)
        parts = fresh
    return jnp.concatenate(parts, axis=1)


def sweep(matrix_ref, swept_ref, panel_of):
    count, order = matrix_ref.shape[:2]
    lane = lax.broadcasted_iota(jnp.int32, (order, order), 1)
    lane_panel = lax.broadcasted_iota(jnp.int32, (count, PANEL, order), 2)
    for start in range(0, order, PANEL):
        rows = slice(start, start + PANEL)
        swept = panel_of(matrix_ref[:, rows, :], start)
        inside_panel = (lane_panel >= start) & (lane_panel < start + PANEL)
        swept_ref[...] = jnp.where(inside_panel, -swept, swept)

        @pl.loop(0, count, unroll=min(count, 8))
        def _(leaf):
            inside = (lane >= start) & (lane < start + PANEL)
            signed = swept_ref[leaf]
            update = mm_exact_t(matrix_ref[leaf, rows, :], signed)
            matrix_ref[leaf] = jnp.where(inside, 0.0, matrix_ref[leaf]) - update
            matrix_ref[leaf, rows, :] = signed


def exchange_kernel(place_ref, label_in_ref, near_ref, base_ref, upper_ref,
                    skeleton_ref, arrived_ref, label_ref, above_ref, below_ref,
                    wide_ref, gain_ref, right_ref, low_ref, packed_ref,
                    matrix_ref, corner_ref, swept_ref, near_sems, upper_sems, label_sems, gain_sems, block_sems):
    count = near_ref.shape[0]
    node, row, mine = lax.axis_index("node"), lax.axis_index("trow"), lax.axis_index("tcol")
    nodes, rows = lax.axis_size("node"), lax.axis_size("trow")
    line = node * rows + row
    lines = nodes * rows

    def at(line_of, col):
        return (line_of // rows, line_of % rows, col)

    next_line, last_line = (line + 1) % lines, (line + lines - 1) % lines
    order = line * SHARE + mine
    following, previous = (order + 1) % (lines * SHARE), (order + lines * SHARE - 1) % (lines * SHARE)
    after, before = at(next_line, mine), at(last_line, mine)
    upper_after = at(following // SHARE, following % SHARE)
    upper_before = at(previous // SHARE, previous % SHARE)
    mates = [at(line, (mine + off) % SHARE) for off in range(1, SHARE)]

    barrier = pltpu.get_barrier_semaphore()
    for device in [after, before, upper_after, upper_before] + mates:
        pl.semaphore_signal(barrier, inc=1, device_id=device, device_id_type=MESH)

    wide_ref[4 : 4 + count] = base_ref[:, :, RANK:]

    label_ref[mine] = label_in_ref[mine]
    pl.semaphore_wait(barrier, 4 + len(mates))

    def remote(src, dst, sems, index, device):
        return pltpu.make_async_remote_copy(
            src_ref=src, dst_ref=dst, send_sem=sems.at[(0,) + index], recv_sem=sems.at[(1,) + index],
            device_id=device, device_id_type=MESH,
        )

    half = pl.ds(RANK, RANK)
    near_copies = [
        remote(base_ref.at[pl.ds(count - 4, 4), :, half], wide_ref.at[pl.ds(0, 4)], near_sems, (0,), after),
        remote(base_ref.at[pl.ds(0, 4), :, half], wide_ref.at[pl.ds(4 + count, 4)], near_sems, (1,), before),
    ]
    for copy in near_copies:
        copy.start()

    def gain_copy(part, col):
        return remote(gain_ref.at[part], gain_ref.at[part], gain_sems, (part,), at(line, col))

    def pass_on(part):
        @pl.when((part < 2) & (mine < SHARE - 1))
        def _():
            gain_copy(part, (mine + 1) % SHARE).start()

        @pl.when((part >= 2) & (mine != 1))
        def _():
            gain_copy(part, (mine + SHARE - 1) % SHARE).start()

    upper_copies = [
        remote(upper_ref.at[:, :, half], above_ref, upper_sems, (0,), upper_after),
        remote(upper_ref.at[:, :, half], below_ref, upper_sems, (1,), upper_before),
    ]
    label_copies = [
        remote(label_in_ref.at[(mine + off) % SHARE], label_ref.at[mine], label_sems, (off - 1,), mates[off - 1])
        for off in range(1, SHARE)
    ]
    for copy in upper_copies + label_copies:
        copy.start()

    @pl.when(mine == 0)
    def _():
        @pl.loop(0, count, unroll=4)
        def _(leaf):
            base = base_ref[leaf]
            turned = mm(near_ref[leaf, 0], base).astype(BF)
            rotated = mm_t(base[:, :RANK], turned)
            corner = rotated[:, :RANK]
            matrix_ref[leaf] = 0.5 * (corner + corner.T)
            corner_ref[leaf] = rotated[:, RANK:].T

        sweep(matrix_ref, swept_ref, sweep_panel)
        for part in (0, 2, 1, 3):
            @pl.loop(0, SHARE, unroll=4)
            def _(owner):
                leaf = owner * SHARE + part
                gain_ref[part, owner] = (-mm_exact(corner_ref[leaf], matrix_ref[leaf])).astype(BF)

            pass_on(part)

    for copy in near_copies:
        copy.wait()

    @pl.loop(0, count, unroll=4)
    def _(leaf):
        base = base_ref[leaf]
        turned = [
            mm(near_ref[leaf, slot], wide_ref[place_ref[leaf, slot]]).astype(BF)
            for slot in range(2)
        ]
        rotated = mm_t(base, jnp.concatenate(turned, axis=1))
        right_ref[leaf] = rotated[:RANK].astype(BF)
        low_ref[leaf] = rotated[RANK:]

    def block_copy(part, off):
        owner = (mine + off) % SHARE
        return remote(packed_ref.at[part, owner], arrived_ref.at[part, mine], block_sems, (part, off - 1), at(line, owner))

    def take(part):
        gain_copy(part, (mine + 1) % SHARE).wait_recv()
        pass_on(part)

    def finish(part):
        @pl.loop(0, SHARE, unroll=4)
        def _(owner):
            leaf = owner * SHARE + part
            fix = mm(gain_ref[part, owner], right_ref[leaf])
            block = low_ref[leaf] - fix
            for slot in range(2):
                columns = slice(slot * RANK, (slot + 1) * RANK)
                skeleton_ref[leaf, slot] = block[:, columns]
                packed_ref[part, owner, slot] = block[:, columns].astype(BF)

        for off in range(1, SHARE):
            block_copy(part, off).start()
        arrived_ref[part, mine] = packed_ref[part, mine]

    shift = 2 * (mine // (SHARE - 1))
    parts = [(part + shift) % SHARE for part in range(SHARE)]

    @pl.when(mine != 0)
    def _():
        take(parts[0])
        take(parts[1])

    @pl.when(mine == 2)
    def _():
        take(parts[2])
        take(parts[3])

    finish(parts[0])
    finish(parts[1])

    @pl.when(mine % 2 == 1)
    def _():
        take(parts[2])

    finish(parts[2])

    @pl.when(mine % 2 == 1)
    def _():
        take(parts[3])

    finish(parts[3])
    for part in parts:
        for off in range(1, SHARE):
            block_copy(part, off).wait()
    for copy in upper_copies + label_copies:
        copy.wait()
    for part in range(SHARE):
        @pl.when((mine < SHARE - 1) if part < 2 else (mine != 1))
        def _():
            gain_copy(part, (mine + 1) % SHARE).wait_send()


def upper_kernel(label_ref, block_ref, base_ref, before_ref, after_ref, out_ref,
                 merged_ref, matrix_ref, swept_ref, right_ref, low_ref):
    parents = base_ref.shape[0]
    merged_ref[...] = jnp.zeros_like(merged_ref)
    for leaf in range(2 * parents):
        for slot in range(8):
            place = (leaf // 2) * 10 + label_ref[slot // 2, 2 * leaf + slot % 2, 0]
            rows = slice((leaf % 2) * RANK, (leaf % 2 + 1) * RANK)
            merged_ref[place, rows, :] = block_ref[leaf, slot // 2, slot % 2]
    for p in range(parents):
        base = base_ref[p]
        for d in range(5):
            left = jnp.concatenate([merged_ref[p * 10 + 2 * d], merged_ref[p * 10 + 2 * d + 1]], axis=1)
            q = p + d - 2
            if d == 2:
                partner = base
            elif q < 0:
                partner = before_ref[q + parents]
            elif q >= parents:
                partner = after_ref[q - parents]
            else:
                partner = base_ref[q, :, RANK:]
            mixed = mm(left, partner).astype(BF)
            lifted = mm_t(base, mixed)
            if d == 2:
                corner = lifted[:RANK, :RANK]
                matrix_ref[p] = 0.5 * (corner + corner.T)
                lifted = lifted[:, RANK:]
            right_ref[p, d] = lifted[:RANK]
            low_ref[p, d] = lifted[RANK:]
    sweep(matrix_ref, swept_ref, sweep_panel_by_four)
    for p in range(parents):
        gain = mm_exact(right_ref[p, 2].T, matrix_ref[p])
        for d in range(5):
            out_ref[p, d] = low_ref[p, d] + mm(gain.astype(BF), right_ref[p, d].astype(BF))


VM = pl.BlockSpec(memory_space=pltpu.VMEM)
SM = pl.BlockSpec(memory_space=pltpu.SMEM)
PARAMS = pltpu.CompilerParams(vmem_limit_bytes=48 * 1024 * 1024)


def shaped(shape, dtype):
    return jax.ShapeDtypeStruct(shape, dtype)


def exchange(place, label, near, base, upper_bases):
    count, parents = near.shape[0], upper_bases.shape[0]
    DMA = pltpu.SemaphoreType.DMA
    return pl.pallas_call(
        exchange_kernel,
        in_specs=[SM] + [VM] * 4,
        out_specs=[VM] * 5,
        out_shape=[
            shaped((count, 2, RANK, RANK), F32),
            shaped((SHARE, SHARE, 2, RANK, RANK), BF),
            shaped((SHARE, 8, RANK), jnp.int32),
            shaped((parents, BLK, RANK), BF),
            shaped((parents, BLK, RANK), BF),
        ],
        scratch_shapes=[
            pltpu.VMEM((count + 8, BLK, RANK), BF),
            pltpu.VMEM((SHARE, SHARE, RANK, RANK), BF),
            pltpu.VMEM((count, RANK, 2 * RANK), BF),
            pltpu.VMEM((count, RANK, 2 * RANK), F32),
            pltpu.VMEM((SHARE, SHARE, 2, RANK, RANK), BF),
            pltpu.VMEM((count, RANK, RANK), F32),
            pltpu.VMEM((count, RANK, RANK), F32),
            pltpu.VMEM((count, PANEL, RANK), F32),
            DMA((2, 2)), DMA((2, 2)), DMA((2, SHARE - 1)), DMA((2, SHARE)), DMA((2, SHARE, SHARE - 1)),
        ],
        compiler_params=pltpu.CompilerParams(
            vmem_limit_bytes=48 * 1024 * 1024, collective_id=0, has_side_effects=True
        ),
        name="exchange",
    )(place, label, near, base, upper_bases)


def upper(target, blocks, base, before, after):
    parents = base.shape[0]
    return pl.pallas_call(
        upper_kernel,
        in_specs=[SM] + [VM] * 4,
        out_specs=VM,
        out_shape=shaped((parents, 5, RANK, RANK), F32),
        scratch_shapes=[
            pltpu.VMEM((parents * 10, 2 * RANK, RANK), BF),
            pltpu.VMEM((parents, RANK, RANK), F32),
            pltpu.VMEM((parents, PANEL, RANK), F32),
            pltpu.VMEM((parents, 5, RANK, RANK), F32),
            pltpu.VMEM((parents, 5, RANK, RANK), F32),
        ],
        compiler_params=PARAMS,
        name="upper",
    )(target, blocks, base, before, after)


def per_device(near_blocks, leaf_bases, upper_bases, neighbours):
    count = near_blocks.shape[0]
    total = count * lax.axis_size(("node", "trow"))
    first_leaf = lax.axis_index(("node", "trow")) * count
    leaf_ids = first_leaf + jnp.arange(count, dtype=jnp.int32)
    target = 2 * ((neighbours // 2 - leaf_ids[:, None] // 2 + 2) % (total // 2)) + neighbours % 2
    label = jnp.broadcast_to(target.reshape(SHARE, 8, 1), (SHARE, 8, RANK))
    place = (neighbours - first_leaf + total // 2) % total - total // 2 + 4
    skeleton, arrived, labels, above, below = exchange(
        place, label, near_blocks, leaf_bases, upper_bases
    )
    upper_skeleton = upper(labels, arrived, upper_bases, above, below)
    return (skeleton, upper_skeleton)


def solution(mesh):
    return jax.shard_map(
        per_device,
        mesh=mesh,
        in_specs=(
            P(("node", "trow"), "tcol", None, None),
            P(("node", "trow"), None, None),
            P(("node", "trow", "tcol"), None, None),
            P(("node", "trow"), "tcol"),
        ),
        out_specs=(
            P(("node", "trow"), "tcol", None, None),
            P(("node", "trow", "tcol"), None, None, None),
        ),
        check_vma=False,
    )
```
